256 devices in a mesh: grp: 4 (over z_lo, core), ctx: 16 (over z_hi, y), wid: 4 (over x).
Axes of the slice: x: 4, y: 4, z: 8 (z_hi: 4, z_lo: 2; z = z_hi * 2 + z_lo), core: 2. Of those that a mesh axis runs over, the one named last changes fastest.
Arguments:
- query: bfloat16 [256, 64, 128], P(None, 'wid'), may hold values from -64 to 64
- keys: bfloat16 [4, 4096, 8, 128], P(None, ('grp', 'ctx'), 'wid'), may hold values from -64 to 64
- values: bfloat16 [4, 4096, 8, 128], P(None, ('grp', 'ctx'), 'wid'), may hold values from -6 to 6
- lengths: int32 [4, 64], replicated, may hold values from 32 to 64
- query_pos: int32 [256], replicated, may hold values from 1024 to 4095
- resid: bfloat16 [256, 5120], P('wid', ('grp', 'ctx')), may hold values from -1.1953125 to 1.1953125
- out_weight: bfloat16 [8192, 5120], P('wid', ('grp', 'ctx')), may hold values from -0.0625 to 0.0625
- enc_weight: bfloat16 [5120, 24576], P('wid', ('grp', 'ctx')), may hold values from -0.078125 to 0.078125
- enc_bias: float32 [24576], P(('grp', 'ctx')), may hold values from -3 to 3
- dec_weight: bfloat16 [24576, 5120], P(('grp', 'ctx'), 'wid'), may hold values from -0.078125 to 0.078125
- dec_bias: float32 [5120], P('wid'), may hold values from -3 to 3
Outputs:
- layer_out: bfloat16 [256, 5120], P('wid', ('grp', 'ctx'))
- enc_grad: bfloat16 [5120, 24576], P('wid', ('grp', 'ctx'))
- enc_bias_grad: float32 [24576], P(('grp', 'ctx'))
- dec_grad: bfloat16 [24576, 5120], P(('grp', 'ctx'), 'wid')
- dec_bias_grad: float32 [5120], P('wid')
The draws below stay inside these ranges and needn't reach their ends.
Inputs may be any that keep to these rules, and one draw needn't show every extreme that they name: `lengths`: live slots of a shard are its first ones.
All inputs are finite; a program needn't handle non-finite values.
Results may differ from the reference program's by a relative error of at most 0.024.
Values may be sent and summed in bfloat16 or wider, within the bound.
No kernel may reach another device: no remote copies, remote signals or barrier semaphores. Data moves between devices by JAX's collectives and lax.ppermute only.
A program may use at most 128 MiB of HBM per device.

```python
import jax
import jax.numpy as jnp
from jax import lax

D = 5120
QH = 64
KVH = 8
HD = 128
LAT = 24576
SEQS = 4
ROWS_SEQ = 64
SLOTS = 64
GQA = 8
SHARDS = 64
CACHE = 4096
ROWS = 256


def query_and_keys(key):
    base = jax.random.fold_in(key, 11)
    key_query, key_keys = jax.random.split(base, 2)
    query = 2.0 * jax.random.normal(key_query, (ROWS, QH, HD), jnp.float32)
    cached = jax.random.normal(key_keys, (SEQS, CACHE, KVH, HD), jnp.float32)
    return (query, cached)


def draw_query(key, part):
    return query_and_keys(key)[0].astype(jnp.bfloat16)


def draw_keys(key, part):
    return query_and_keys(key)[1].astype(jnp.bfloat16)


def plant(result, rng, low, high):
    spot = [jax.random.randint(jax.random.fold_in(rng, axis), (), 0, length) for axis, length in enumerate(result.shape)]
    main_axis = result.shape.index(max(result.shape))
    neighbour = spot[:main_axis] + [(spot[main_axis] + 1) % result.shape[main_axis]] + spot[main_axis + 1:]
    return result.at[tuple(spot)].set(low).at[tuple(neighbour)].set(high)


def block_levels(stream_key, extent, pieces, least, largest):
    loudness, own = 1.0, jax.random.fold_in(stream_key, 6)
    for dim, blocks in pieces:
        steps = jnp.exp(jax.random.uniform(jax.random.fold_in(own, dim), (blocks,), jnp.float32, least / len(pieces), largest / len(pieces)))
        loudness = loudness * jnp.repeat(steps, extent[dim] // blocks).reshape([-1 if axis == dim else 1 for axis in range(len(extent))])
    return loudness


def normal_values(rng, shape, spread, bound, cuts=(), kind=jnp.bfloat16):
    loudness = block_levels(rng, shape, cuts, -0.22, 0.18) if cuts else 1.0
    drawn = jax.random.normal(rng, shape, jnp.float32) * spread * loudness
    return jnp.minimum(jnp.maximum(drawn, -bound), bound).astype(kind)


def setup_inputs(seed: int = 0) -> dict:
    arg_keys = jax.random.split(jax.random.key(seed), 12)
    return {
        "query": draw_query(jax.random.fold_in(arg_keys[11], 71), 0),
        "keys": draw_keys(jax.random.fold_in(arg_keys[11], 71), 0),
        "values": normal_values(arg_keys[2], (SEQS, CACHE, KVH, HD), 1.0, 6.0, ((1, 64), (2, 4))),
        "lengths": plant(jax.random.randint(arg_keys[3], (SEQS, SHARDS), SLOTS // 2, SLOTS + 1), jax.random.fold_in(arg_keys[3], 1), SLOTS // 2, SLOTS).astype(jnp.int32),
        "query_pos": plant(jax.random.randint(arg_keys[4], (ROWS,), SHARDS * SLOTS // 4, SHARDS * SLOTS), jax.random.fold_in(arg_keys[4], 1), SHARDS * SLOTS // 4, (SHARDS * SLOTS) - 1).astype(jnp.int32),
        "resid": normal_values(arg_keys[5], (ROWS, D), 0.2, 1.1953125, ((0, 4), (1, 64))),
        "out_weight": normal_values(arg_keys[6], (QH * HD, D), (QH * HD) ** -0.5, 0.0625, ((0, 4), (1, 64))),
        "enc_weight": normal_values(arg_keys[7], (D, LAT), D ** -0.5, 0.078125, ((0, 4), (1, 64))),
        "enc_bias": normal_values(arg_keys[8], (LAT,), 0.5, 3.0, ((0, 64),), jnp.float32),
        "dec_weight": normal_values(arg_keys[9], (LAT, D), D ** -0.5, 0.078125, ((0, 64), (1, 4))),
        "dec_bias": normal_values(arg_keys[10], (D,), 0.5, 3.0, ((0, 4),), jnp.float32),
    }


def one_sequence(items):
    q_seq, k_seq, v_seq, key_pos, live_slot, row_position = items
    scores = jnp.einsum("rkgd,tkd->krgt", q_seq.astype(jnp.float32), k_seq.astype(jnp.float32),
                        precision=lax.Precision.HIGHEST) * (HD ** -0.5)
    visible = live_slot[None, :] & (key_pos[None, :] <= row_position[:, None])
    visible_mask = visible[None, :, None, :]
    peak = jnp.max(jnp.where(visible_mask, scores, -1e30), axis=-1)
    weights = jnp.where(visible_mask, jnp.exp(scores - peak[..., None]), 0.0)
    weight_sum = jnp.sum(weights, axis=-1)
    weights_low = lax.optimization_barrier(weights.astype(jnp.bfloat16)).astype(jnp.float32)
    weighted = jnp.einsum("krgt,tkd->rkgd", weights_low, v_seq.astype(jnp.float32),
                          precision=lax.Precision.HIGHEST)
    return weighted / jnp.transpose(weight_sum, (1, 0, 2))[..., None]


def reference(query, keys, values, lengths, query_pos, resid, out_weight, enc_weight, enc_bias, dec_weight, dec_bias):
    slot_ids = jnp.arange(SLOTS, dtype=jnp.int32)
    offsets = (jnp.cumsum(lengths, axis=1) - lengths).astype(jnp.int32)
    key_pos = (offsets[:, :, None] + slot_ids[None, None, :]).astype(jnp.int32).reshape(SEQS, CACHE)
    live_slot = (slot_ids[None, None, :] < lengths[:, :, None]).reshape(SEQS, CACHE)
    q_view = query.reshape(SEQS, ROWS_SEQ, KVH, GQA, HD)
    row_position = query_pos.reshape(SEQS, ROWS_SEQ)
    attn = lax.map(one_sequence, (q_view, keys, values, key_pos, live_slot, row_position))
    attention = attn.astype(jnp.bfloat16).reshape(ROWS, QH * HD)
    layer_out = (jnp.dot(attention, out_weight, preferred_element_type=jnp.float32)
                 + resid.astype(jnp.float32)).astype(jnp.bfloat16)
    preact = jnp.dot(layer_out, enc_weight, preferred_element_type=jnp.float32) + enc_bias
    latents = (jax.nn.softplus(4.0 * preact) * 0.25).astype(jnp.bfloat16)
    recon = jnp.dot(latents, dec_weight, preferred_element_type=jnp.float32)
    scaled_error = ((recon + dec_bias - layer_out.astype(jnp.float32)) * (ROWS ** -0.5)).astype(jnp.bfloat16)
    dec_grad = lax.dot_general(latents, scaled_error, (((0,), (0,)), ((), ())),
                               preferred_element_type=jnp.float32).astype(jnp.bfloat16)
    dec_bias_grad = jnp.sum(scaled_error.astype(jnp.float32), axis=0)
    latent_grad = lax.dot_general(scaled_error, dec_weight, (((1,), (1,)), ((), ())),
                                  preferred_element_type=jnp.float32)
    preact_grad = (latent_grad * jax.nn.sigmoid(4.0 * preact)).astype(jnp.bfloat16)
    enc_grad = lax.dot_general(layer_out, preact_grad, (((0,), (0,)), ((), ())),
                               preferred_element_type=jnp.float32).astype(jnp.bfloat16)
    enc_bias_grad = jnp.sum(preact_grad.astype(jnp.float32), axis=0)
    return layer_out, enc_grad, enc_bias_grad, dec_grad, dec_bias_grad
```

```python
import jax
import jax.numpy as jnp
from jax import lax
from jax.sharding import Mesh
from jax.sharding import PartitionSpec as P

HD = 128
ZL, CO, ZH, Y, X = ("zl", "co", "zh", "y", "x")
SHARD = (ZL, CO, ZH, Y)
F32, BF16 = (jnp.float32, jnp.bfloat16)


def other_core(a):
    return lax.ppermute(a, CO, [(0, 1), (1, 0)])


def shifted(a, axis, k):
    n = lax.axis_size(axis)
    return lax.ppermute(a, axis, [(i, (i + k) % n) for i in range(n)])


def exchanged(a, axes):
    return lax.all_to_all(a, axes, 0, 0, tiled=True)


def gathered(a, axes):
    return exchanged(jnp.broadcast_to(a, (lax.axis_size(axes), *a.shape)), axes)


def rounded(a):
    return lax.reduce_precision(a, exponent_bits=8, mantissa_bits=7)


def dot(a, b, contract):
    return lax.dot_general(a, b, (contract, ((), ())), preferred_element_type=F32)


def body(
    query,
    keys,
    values,
    lengths,
    query_pos,
    resid,
    out_weight,
    enc_weight,
    enc_bias,
    dec_weight,
    dec_bias,
):
    zl, co, zh, y, x = (lax.axis_index(name) for name in (ZL, CO, ZH, Y, X))
    seqs, slots, kv_local, head_dim = keys.shape
    rows = query.shape[0]
    heads = query.shape[1]
    group = heads // kv_local
    half = rows // seqs // 2
    width = kv_local * head_dim
    cols = out_weight.shape[1]
    lat = enc_weight.shape[1]
    feats = enc_weight.shape[0]

    kv = jnp.concatenate(
        [keys.reshape(seqs, slots, width), values.reshape(seqs, slots, width)], axis=1
    )
    kv = exchanged(kv, Y)
    kv = jnp.stack([kv, other_core(kv)])
    shards = 2 * seqs
    k_all = kv[:, :, :slots].reshape(shards * slots, kv_local, head_dim)
    v_all = kv[:, :, slots:].reshape(shards * slots, kv_local, head_dim)

    both = jnp.concatenate([out_weight, resid], axis=0).T
    ring = jnp.stack([both] + [shifted(both, Y, k) for k in (1, 2, 3)])
    proj_mine = jnp.concatenate(
        [lax.dynamic_index_in_dim(ring, (y - j) % 4, 0, keepdims=False) for j in range(4)], axis=0
    )
    proj_other = other_core(proj_mine)
    enc_other = other_core(enc_weight)
    dec_other = other_core(dec_weight)
    bias_both = jnp.concatenate([enc_bias, other_core(enc_bias)])

    first = 2 * half * y + half * co
    q = lax.dynamic_slice_in_dim(query, first, half, 0)
    q = q.reshape(half, kv_local, group, head_dim).transpose(1, 2, 0, 3)
    q = q.reshape(kv_local, group * half, head_dim)
    lens = lax.dynamic_index_in_dim(lengths, y, 0, keepdims=False)
    ids = jnp.arange(lens.shape[0], dtype=jnp.int32)
    offsets = jnp.sum(jnp.where(ids[None, :] < ids[:, None], lens[None, :], 0), axis=1)
    slot_ids = jnp.arange(slots, dtype=jnp.int32)

    def positions(c):
        start = ((zl * 2 + c) * 4 + zh) * 4
        own_offset = lax.dynamic_slice_in_dim(offsets, start, 4, 0)
        own_len = lax.dynamic_slice_in_dim(lens, start, 4, 0)
        return jnp.where(
            slot_ids[None, :] < own_len[:, None], own_offset[:, None] + slot_ids[None, :], 1 << 30
        )

    key_pos = jnp.stack([positions(co), positions(1 - co)]).reshape(-1)
    row_pos = lax.dynamic_slice_in_dim(query_pos, first, half, 0)
    visible = key_pos[None, :] <= row_pos[:, None]
    visible = jnp.broadcast_to(visible[None, None], (kv_local, group, half, shards * slots))
    visible = visible.reshape(kv_local, group * half, shards * slots)
    scores = jnp.einsum("kqd,tkd->kqt", q, k_all, preferred_element_type=F32) * HD ** (-0.5)
    peak = jnp.max(jnp.where(visible, scores, -1e30), axis=-1)
    weights = jnp.where(visible, jnp.exp(scores - peak[..., None]), 0.0)
    weight_sum = jnp.sum(weights, axis=-1)
    weighted = jnp.einsum("kqt,tkd->kqd", weights.astype(BF16), v_all, preferred_element_type=F32)
    some = weight_sum > 0.0
    safe = jnp.where(some, weight_sum, 1.0)
    level = jnp.where(some, peak + jnp.log(safe), -1e30)
    high = rounded(level)
    mid = rounded(level - high)
    low = rounded(level - high - mid)
    extras = jnp.stack([high, mid, low], axis=-1).astype(BF16)
    extras = jnp.pad(extras, ((0, 0), (0, 0), (0, HD - 3)))
    payload = jnp.concatenate([(weighted / safe[..., None]).astype(BF16), extras], axis=-1)
    payload = exchanged(payload.reshape(8, 2 * half, 2 * HD), (ZL, ZH)).astype(F32)
    level = payload[:, :, HD] + payload[:, :, HD + 1] + payload[:, :, HD + 2]
    share = jnp.exp(level - jnp.max(level, axis=0))
    attention = jnp.sum(payload[:, :, :HD] * share[..., None], axis=0)
    attention = (attention / jnp.sum(share, axis=0)[..., None]).astype(BF16)
    attention = gathered(attention, (ZL, ZH))
    attention = attention.reshape(heads, half, HD).transpose(1, 0, 2).reshape(half, heads * HD)

    def projected(proj):
        out = dot(attention, proj[:, : heads * HD], ((1,), (1,)))
        res = lax.dynamic_slice_in_dim(proj[:, heads * HD :], half * co, half, 1)
        return (out + jnp.where(x == y, res.astype(F32).T, 0.0)).astype(BF16)

    mine, others = (projected(proj_mine), projected(proj_other))
    part = jnp.stack([jnp.where(co == 0, mine, others), jnp.where(co == 0, others, mine)])
    part = part.reshape(2, 2, half // 2, 4 * cols).transpose(1, 0, 2, 3)
    part = jnp.where(jnp.arange(2)[None, :, None, None, None] == zl, part[:, None], 0)
    part = exchanged(part.reshape(8, half // 2, 4 * cols), (ZL, X))
    piece = jnp.sum(part.astype(F32), axis=0).astype(BF16)

    block = gathered(piece, (ZH, Y, ZL)).reshape(4, seqs * half, 4 * cols)
    my_rows = seqs * half

    def encoded(weight):
        return jnp.einsum(
            "zrf,zfc->rc", block, weight.reshape(4, feats // 4, lat), preferred_element_type=F32
        )

    part = jnp.concatenate([encoded(enc_weight), encoded(enc_other)], axis=1)
    low = part.astype(BF16)
    preact = part + sum(shifted(low, X, k).astype(F32) for k in (1, 2, 3)) + bias_both
    latents = (jax.nn.softplus(4.0 * preact) * 0.25).astype(BF16)

    block_other = other_core(block)
    latents_other = other_core(latents[:, lat:])
    halves = [lax.dynamic_index_in_dim(b, zh, 0, keepdims=False) for b in (block, block_other)]
    halves = [
        lax.dynamic_slice(b, (half * (2 * zl + co), cols * y), (half, cols)) for b in halves
    ]
    halves = [jnp.where(co == 0, halves[0], halves[1]), jnp.where(co == 0, halves[1], halves[0])]
    layer_out = lax.ppermute(
        jnp.concatenate(halves, axis=0),
        (ZL, CO, X),
        [(b * 4 + a, a * 4 + b) for a in range(4) for b in range(4)],
    )

    wide = feats // 2
    few = my_rows // 16

    def decoded(k):
        piece = slice(k * wide, (k + 1) * wide)
        return dot(latents[:, :lat], dec_weight[:, piece], ((1,), (0,))) + dot(
            latents[:, lat:], dec_other[:, piece], ((1,), (0,))
        )

    recon = jnp.stack([decoded(0), decoded(1)]).astype(BF16).reshape(32, few, wide)
    recon = jnp.sum(exchanged(recon, (ZL, ZH, Y)).astype(F32), axis=0)
    at = (zl * 4 + zh) * 4 + y
    natural = block.transpose(1, 0, 2).reshape(my_rows, feats)
    target = lax.dynamic_slice(natural, (few * (at % 16), wide * (at // 16)), (few, wide))
    target_bias = lax.dynamic_slice_in_dim(dec_bias, wide * (at // 16), wide, 0)
    error = ((recon + target_bias - target.astype(F32)) * rows ** (-0.5)).astype(BF16)
    error = gathered(error, (ZL, ZH, Y)).reshape(2, my_rows, wide)
    error_other = other_core(error)

    def pulled(weight):
        return sum(
            dot(error[k], weight[:, k * wide : (k + 1) * wide], ((1,), (1,))) for k in (0, 1)
        )

    part = jnp.concatenate([pulled(dec_weight), pulled(dec_other)], axis=1)
    low = part.astype(BF16)
    latent_grad = part + sum(shifted(low, X, k).astype(F32) for k in (1, 2, 3))
    preact_grad = (latent_grad * jax.nn.sigmoid(4.0 * preact)).astype(BF16)
    preact_grad_other = other_core(preact_grad[:, lat:])
    preact_grad = preact_grad[:, :lat]

    all_latents = jnp.concatenate([latents[:, :lat], latents_other], axis=0)
    all_error = jnp.concatenate([error, error_other], axis=1)
    all_error = all_error.transpose(1, 0, 2).reshape(rows, feats)
    dec_grad = dot(all_latents, all_error, ((0,), (0,))).astype(BF16)
    dec_bias_grad = jnp.sum(all_error, axis=0, dtype=F32)
    all_grad = jnp.concatenate([preact_grad, preact_grad_other], axis=0)
    all_block = jnp.concatenate([block, block_other], axis=1)
    enc_grad = jnp.einsum("zrf,rc->zfc", all_block, all_grad, preferred_element_type=F32)
    enc_grad = enc_grad.astype(BF16).reshape(feats, lat)
    enc_bias_grad = jnp.sum(all_grad, axis=0, dtype=F32)
    return (layer_out, enc_grad, enc_bias_grad, dec_grad, dec_bias_grad)


def solution(mesh):
    torus = Mesh(mesh.devices.reshape(2, 2, 4, 4, mesh.shape["wid"]), (ZL, CO, ZH, Y, X))
    in_specs = (
        P(None, X, None),
        P(None, SHARD, X, None),
        P(None, SHARD, X, None),
        P(),
        P(),
        P(X, SHARD),
        P(X, SHARD),
        P(X, SHARD),
        P(SHARD),
        P(SHARD, X),
        P(X),
    )
    out_specs = (P(X, SHARD), P(X, SHARD), P(SHARD), P(SHARD, X), P(X))
    return jax.shard_map(body, mesh=torus, in_specs=in_specs, out_specs=out_specs, check_vma=False)
```

```python
import jax
import jax.numpy as jnp
from jax import lax
from jax.experimental import pallas as pl
from jax.experimental.pallas import tpu as pltpu
from jax.sharding import Mesh
from jax.sharding import PartitionSpec as P

HD = 128
ZL, CO, ZH, Y, X = ("zl", "co", "zh", "y", "x")
SHARD = (ZL, CO, ZH, Y)
F32, BF16 = (jnp.float32, jnp.bfloat16)


def other_core(a):
    return lax.ppermute(a, CO, [(0, 1), (1, 0)])


def shifted(a, axis, k):
    n = lax.axis_size(axis)
    return lax.ppermute(a, axis, [(i, (i + k) % n) for i in range(n)])


def exchanged(a, axes):
    return lax.all_to_all(a, axes, 0, 0, tiled=True)


def gathered(a, axes):
    return exchanged(jnp.broadcast_to(a, (lax.axis_size(axes), *a.shape)), axes)


def dot(a, b, contract):
    return lax.dot_general(a, b, (contract, ((), ())), preferred_element_type=F32)


def attend(q_ref, kv_ref, other_ref, key_ref, row_ref, out_ref):
    slots = kv_ref.shape[1] // 2
    visible = key_ref[...] <= row_ref[...]
    lane = lax.broadcasted_iota(jnp.int32, (q_ref.shape[1], HD), 1)
    for k in range(q_ref.shape[0]):
        across = slice(k * HD, (k + 1) * HD)
        keys, values = (
            jnp.concatenate([ref[j, lo : lo + slots, across] for ref in (kv_ref, other_ref) for j in range(4)])
            for lo in (0, slots)
        )
        scores = dot(q_ref[k], keys, ((1,), (1,))) * HD ** (-0.5)
        peak = jnp.max(jnp.where(visible, scores, -1e30), axis=1, keepdims=True)
        weights = jnp.where(visible, jnp.exp(scores - peak), 0.0)
        weight_sum = jnp.sum(weights, axis=1, keepdims=True)
        weighted = dot(weights.astype(BF16), values, ((1,), (0,)))
        some = weight_sum > 0.0
        safe = jnp.where(some, weight_sum, 1.0)
        level = jnp.where(some, peak + jnp.log(safe), -1e30)
        high = level.astype(BF16).astype(F32)
        mid = (level - high).astype(BF16).astype(F32)
        low = level - high - mid
        extra = jnp.where(lane == 0, high, jnp.where(lane == 1, mid, jnp.where(lane == 2, low, 0.0)))
        parts = out_ref.shape[0] // q_ref.shape[0]
        where = slice(k * parts, (k + 1) * parts)
        out_ref[where, :, :HD] = (weighted / safe).astype(BF16).reshape(parts, -1, HD)
        out_ref[where, :, HD:] = extra.astype(BF16).reshape(parts, -1, HD)


def project(core_ref, message_ref, mine_ref, other_ref, res_mine_ref, res_other_ref, out_ref):
    message = message_ref[...].astype(F32)
    level = jnp.sum(message[:, :, HD:], axis=2, keepdims=True)
    share = jnp.exp(level - jnp.max(level, axis=0, keepdims=True))
    attention = jnp.sum(message[:, :, :HD] * share, axis=0) / jnp.sum(share, axis=0)
    half = attention.shape[0] // 2
    attention = jnp.concatenate([attention[:half], attention[half:]], axis=1).astype(BF16)
    core = core_ref[0]
    wide = out_ref.shape[-1]
    for high in range(2):
        for weight, res, low in ((mine_ref, res_mine_ref, core), (other_ref, res_other_ref, 1 - core)):
            out = dot(attention, weight[high], ((1,), (1,))) + res[high].astype(F32)
            out = out.astype(BF16)
            for cb in range(2):
                for rb in range(4):
                    out_ref[cb, rb, 2 * high + low] = out[8 * rb : 8 * rb + 8, wide * cb : wide * (cb + 1)]


def body(
    query,
    keys,
    values,
    lengths,
    query_pos,
    resid,
    out_weight,
    enc_weight,
    enc_bias,
    dec_weight,
    dec_bias,
):
    zl, co, zh, y, x = (lax.axis_index(name) for name in (ZL, CO, ZH, Y, X))
    seqs, slots, kv_local, head_dim = keys.shape
    rows = query.shape[0]
    heads = query.shape[1]
    group = heads // kv_local
    half = rows // seqs // 2
    width = kv_local * head_dim
    cols = out_weight.shape[1]
    lat = enc_weight.shape[1]
    feats = enc_weight.shape[0]

    kv = jnp.concatenate(
        [keys.reshape(seqs, slots, width), values.reshape(seqs, slots, width)], axis=1
    )
    own = lax.dynamic_index_in_dim(kv, y, 0, keepdims=False)
    kv = [own] + [
        shifted(lax.dynamic_index_in_dim(kv, (y + k) % 4, 0, keepdims=False), Y, k)
        for k in (1, 2, 3)
    ]
    kv = jnp.stack(kv)
    kv_other = other_core(kv)

    proj = out_weight.reshape(8, 2 * HD, cols).transpose(0, 2, 1)
    res = jnp.pad(resid.reshape(8, 8, cols), ((0, 0), (0, 8), (0, 2 * HD - cols)))
    proj = exchanged(jnp.concatenate([proj, res], axis=1), (ZL, ZH))
    proj, kv, kv_other = lax.optimization_barrier((proj, kv, kv_other))
    ring = jnp.stack([proj] + [shifted(proj, Y, k) for k in (1, 2, 3)])
    ring = jnp.stack(
        [lax.dynamic_index_in_dim(ring, (y - j) % 4, 0, keepdims=False) for j in range(4)], axis=1
    )
    ring_other = other_core(ring)
    at = zl * 4 + zh

    def split(ring):
        weight = ring[:, :, :cols].reshape(2, feats, 2 * HD)
        res = ring[:, :, cols : cols + 8, :cols].reshape(2, 4, 4, 8, cols)
        res = res.transpose(0, 3, 1, 2, 4).reshape(2, 1, 8, feats)
        here = (jnp.arange(4) == at % 4) & (x == y) & (co == at // 4)
        return weight, jnp.where(here[None, :, None, None], res, 0).reshape(2, half, feats)

    proj_mine, res_mine = split(ring)
    proj_other, res_other = split(ring_other)
    enc_other = other_core(enc_weight)
    dec_other = other_core(dec_weight)
    bias_both = jnp.concatenate([enc_bias, other_core(enc_bias)])

    first = 2 * half * y + half * co
    q = lax.dynamic_slice_in_dim(query, first, half, 0)
    q = q.reshape(half, kv_local, group, head_dim).transpose(1, 2, 0, 3)
    q = q.reshape(kv_local, group * half, head_dim)
    lens = lax.dynamic_index_in_dim(lengths, y, 0, keepdims=False)
    ids = jnp.arange(lens.shape[0], dtype=jnp.int32)
    offsets = jnp.sum(jnp.where(ids[None, :] < ids[:, None], lens[None, :], 0), axis=1)
    slot_ids = jnp.arange(slots, dtype=jnp.int32)
    turn = (y - jnp.arange(4)) % 4
    shard = ((zl * 2 + jnp.stack([co, 1 - co])[:, None]) * 4 + zh) * 4 + turn[None, :]
    pick = shard[..., None] == ids
    own_offset = jnp.sum(jnp.where(pick, offsets, 0), axis=-1)[..., None]
    own_len = jnp.sum(jnp.where(pick, lens, 0), axis=-1)[..., None]
    key_pos = jnp.where(slot_ids < own_len, own_offset + slot_ids, 1 << 30)
    row_pos = lax.dynamic_slice_in_dim(query_pos, first, half, 0)
    row_pos = jnp.broadcast_to(row_pos[None, :], (group, half)).reshape(-1, 1)

    message = pl.pallas_call(
        attend, out_shape=jax.ShapeDtypeStruct((8, 2 * half, 2 * HD), BF16), name="attend"
    )(q, kv, kv_other, key_pos.reshape(1, -1), row_pos)
    message = exchanged(message, (ZL, ZH))
    part = pl.pallas_call(
        project,
        out_shape=jax.ShapeDtypeStruct((2, 4, 4, 8, feats // 2), BF16),
        in_specs=[pl.BlockSpec(memory_space=pltpu.SMEM)]
        + [pl.BlockSpec(memory_space=pltpu.VMEM)] * 5,
        compiler_params=pltpu.CompilerParams(vmem_limit_bytes=32 * 2**20),
        name="project",
    )(co.reshape(1), message, proj_mine, proj_other, res_mine, res_other)
    part = exchanged(part.reshape(32, 8, feats // 2), (ZL, ZH, X))
    piece = jnp.sum(part.astype(F32), axis=0).astype(BF16)

    my_rows = seqs * half
    wide = feats // 2
    few = my_rows // 16
    block = gathered(piece, (ZL, Y, ZH)).reshape(2, my_rows, wide)

    def encoded(weight):
        return jnp.einsum(
            "zrf,zfc->rc", block, weight.reshape(2, wide, lat), preferred_element_type=F32
        )

    part = jnp.concatenate([encoded(enc_weight), encoded(enc_other)], axis=1)
    low = part.astype(BF16)
    preact = part + sum(shifted(low, X, k).astype(F32) for k in (1, 2, 3)) + bias_both
    latents = (jax.nn.softplus(4.0 * preact) * 0.25).astype(BF16)

    block_other = other_core(block)
    latents_other = other_core(latents[:, lat:])
    halves = [lax.dynamic_index_in_dim(b, zh // 2, 0, keepdims=False) for b in (block, block_other)]
    spot = (half * (2 * zl + co), 4 * cols * (zh % 2) + cols * y)
    halves = [lax.dynamic_slice(b, spot, (half, cols)) for b in halves]
    halves = [jnp.where(co == 0, halves[0], halves[1]), jnp.where(co == 0, halves[1], halves[0])]
    layer_out = lax.ppermute(
        jnp.concatenate(halves, axis=0),
        (ZL, CO, X),
        [(b * 4 + a, a * 4 + b) for a in range(4) for b in range(4)],
    )

    def decoded(k):
        piece = slice(k * wide, (k + 1) * wide)
        return dot(latents[:, :lat], dec_weight[:, piece], ((1,), (0,))) + dot(
            latents[:, lat:], dec_other[:, piece], ((1,), (0,))
        )

    recon = jnp.stack([decoded(0), decoded(1)]).astype(BF16).reshape(32, few, wide)
    recon = jnp.sum(exchanged(recon, (ZL, Y, ZH)).astype(F32), axis=0)
    target_bias = lax.dynamic_slice_in_dim(dec_bias, wide * zl, wide, 0)
    error = ((recon + target_bias - piece.astype(F32)) * rows ** (-0.5)).astype(BF16)
    error = gathered(error, (ZL, Y, ZH)).reshape(2, my_rows, wide)
    error_other = other_core(error)

    def pulled(weight):
        return sum(
            dot(error[k], weight[:, k * wide : (k + 1) * wide], ((1,), (1,))) for k in (0, 1)
        )

    part = jnp.concatenate([pulled(dec_weight), pulled(dec_other)], axis=1)
    low = part.astype(BF16)
    latent_grad = part + sum(shifted(low, X, k).astype(F32) for k in (1, 2, 3))
    preact_grad = (latent_grad * jax.nn.sigmoid(4.0 * preact)).astype(BF16)
    preact_grad_other = other_core(preact_grad[:, lat:])
    preact_grad = preact_grad[:, :lat]

    all_latents = jnp.concatenate([latents[:, :lat], latents_other], axis=0)
    all_error = jnp.concatenate([error, error_other], axis=1)
    all_error = all_error.transpose(1, 0, 2).reshape(rows, feats)
    dec_grad = dot(all_latents, all_error, ((0,), (0,))).astype(BF16)
    dec_bias_grad = jnp.sum(all_error, axis=0, dtype=F32)
    all_grad = jnp.concatenate([preact_grad, preact_grad_other], axis=0)
    all_block = jnp.concatenate([block, block_other], axis=1)
    enc_grad = jnp.einsum("zrf,rc->zfc", all_block, all_grad, preferred_element_type=F32)
    enc_grad = enc_grad.astype(BF16).reshape(feats, lat)
    enc_bias_grad = jnp.sum(all_grad, axis=0, dtype=F32)
    return (layer_out, enc_grad, enc_bias_grad, dec_grad, dec_bias_grad)


def solution(mesh):
    torus = Mesh(mesh.devices.reshape(2, 2, 4, 4, mesh.shape["wid"]), (ZL, CO, ZH, Y, X))
    in_specs = (
        P(None, X, None),
        P(None, SHARD, X, None),
        P(None, SHARD, X, None),
        P(),
        P(),
        P(X, SHARD),
        P(X, SHARD),
        P(X, SHARD),
        P(SHARD),
        P(SHARD, X),
        P(X),
    )
    out_specs = (P(X, SHARD), P(X, SHARD), P(SHARD), P(SHARD, X), P(X))
    return jax.shard_map(body, mesh=torus, in_specs=in_specs, out_specs=out_specs, check_vma=False)
```

```python
import jax
import jax.numpy as jnp
from jax import lax
from jax.experimental import pallas as pl
from jax.experimental.pallas import tpu as pltpu
from jax.sharding import Mesh
from jax.sharding import PartitionSpec as P

HD = 128
ZL, CO, ZH, Y, X = ("zl", "co", "zh", "y", "x")
SHARD = (ZL, CO, ZH, Y)
F32, BF16 = (jnp.float32, jnp.bfloat16)


def other_core(a):
    return lax.ppermute(a, CO, [(0, 1), (1, 0)])


def shifted(a, axis, k):
    n = lax.axis_size(axis)
    return lax.ppermute(a, axis, [(i, (i + k) % n) for i in range(n)])


def exchanged(a, axes):
    return lax.all_to_all(a, axes, 0, 0, tiled=True)


def gathered(a, axes):
    return exchanged(jnp.broadcast_to(a, (lax.axis_size(axes), *a.shape)), axes)


def dot(a, b, contract):
    return lax.dot_general(a, b, (contract, ((), ())), preferred_element_type=F32)


def attend(q_ref, kv_ref, other_ref, key_ref, row_ref, out_ref):
    slots = kv_ref.shape[1] // 2
    visible = key_ref[...] <= row_ref[...]
    lane = lax.broadcasted_iota(jnp.int32, (q_ref.shape[1], HD), 1)
    for k in range(q_ref.shape[0]):
        across = slice(k * HD, (k + 1) * HD)
        keys, values = (
            jnp.concatenate([ref[j, lo : lo + slots, across] for ref in (kv_ref, other_ref) for j in range(4)])
            for lo in (0, slots)
        )
        scores = dot(q_ref[k], keys, ((1,), (1,))) * HD ** (-0.5)
        peak = jnp.max(jnp.where(visible, scores, -1e30), axis=1, keepdims=True)
        weights = jnp.where(visible, jnp.exp(scores - peak), 0.0)
        weight_sum = jnp.sum(weights, axis=1, keepdims=True)
        weighted = dot(weights.astype(BF16), values, ((1,), (0,)))
        some = weight_sum > 0.0
        safe = jnp.where(some, weight_sum, 1.0)
        level = jnp.where(some, peak + jnp.log(safe), -1e30)
        high = level.astype(BF16).astype(F32)
        mid = (level - high).astype(BF16).astype(F32)
        low = level - high - mid
        extra = jnp.where(lane == 0, high, jnp.where(lane == 1, mid, jnp.where(lane == 2, low, 0.0)))
        parts = out_ref.shape[0] // q_ref.shape[0]
        where = slice(k * parts, (k + 1) * parts)
        out_ref[where, :, :HD] = (weighted / safe).astype(BF16).reshape(parts, -1, HD)
        out_ref[where, :, HD:] = extra.astype(BF16).reshape(parts, -1, HD)


def combine(message_ref, out_ref):
    message = message_ref[...].astype(F32)
    level = jnp.sum(message[:, :, HD:], axis=2, keepdims=True)
    share = jnp.exp(level - jnp.max(level, axis=0, keepdims=True))
    attention = jnp.sum(message[:, :, :HD] * share, axis=0) / jnp.sum(share, axis=0)
    half = attention.shape[0] // 2
    out_ref[:, :HD] = attention[:half].astype(BF16)
    out_ref[:, HD:] = attention[half:].astype(BF16)


def project(at_ref, a_ref, b_ref, c_ref, d_ref, mine_ref, other_ref, res_mine_ref, res_other_ref, out_ref):
    attention = jnp.concatenate([ref[...] for ref in (a_ref, b_ref, c_ref, d_ref)])
    few, cols = (out_ref.shape[2], out_ref.shape[3] // 4)
    turn, core = (at_ref[0], at_ref[1])
    for high in range(2):
        for ref, res, low in ((mine_ref, res_mine_ref, core), (other_ref, res_other_ref, 1 - core)):
            weight = jnp.concatenate([ref[4 * high + j, :cols] for j in range(4)])
            out = dot(attention, weight, ((1,), (1,))) + res[high].astype(F32)
            out = out.astype(BF16)
            for k in range(4):
                seq = lax.rem(turn - k + 4, 4)
                for r in range(2):
                    start = few * (2 * k + r)
                    out_ref[2 * seq + r, 2 * high + low] = out[start : start + few]


def body(
    query,
    keys,
    values,
    lengths,
    query_pos,
    resid,
    out_weight,
    enc_weight,
    enc_bias,
    dec_weight,
    dec_bias,
):
    zl, co, zh, y, x = (lax.axis_index(name) for name in (ZL, CO, ZH, Y, X))
    seqs, slots, kv_local, head_dim = keys.shape
    rows = query.shape[0]
    heads = query.shape[1]
    group = heads // kv_local
    half = rows // seqs // 2
    width = kv_local * head_dim
    cols = out_weight.shape[1]
    lat = enc_weight.shape[1]
    feats = enc_weight.shape[0]

    kv = jnp.concatenate(
        [keys.reshape(seqs, slots, width), values.reshape(seqs, slots, width)], axis=1
    )
    ring = [lax.dynamic_index_in_dim(kv, zh, 0, keepdims=False)] + [
        shifted(lax.dynamic_index_in_dim(kv, (zh + k) % 4, 0, keepdims=False), ZH, k)
        for k in (1, 2, 3)
    ]

    proj = out_weight.reshape(8, 2 * HD, cols).transpose(0, 2, 1)
    res = jnp.pad(resid.reshape(8, 8, cols), ((0, 0), (0, 8), (0, 2 * HD - cols)))
    proj = jnp.concatenate([proj, res], axis=1)
    ring[1], proj = lax.optimization_barrier((ring[1], proj))
    proj_mine = exchanged(proj, (ZL, Y))
    kv = jnp.stack(ring)
    kv_other = other_core(kv)
    proj_other = other_core(proj_mine)
    at = zl * 4 + y
    turn = (zh - jnp.arange(4)) % 4

    def residual(proj):
        res = proj[:, cols : cols + 8, :cols].reshape(2, 4, 8, cols)
        res = res.transpose(0, 2, 1, 3).reshape(2, 1, 1, 8, 4 * cols)
        here = (jnp.arange(4) == at % 4) & (turn == x)[:, None] & (co == at // 4)
        return jnp.where(here[None, :, :, None, None], res, 0).reshape(2, seqs * half, 4 * cols)

    res_mine, res_other = (residual(proj_mine), residual(proj_other))
    enc_other = other_core(enc_weight)
    dec_other = other_core(dec_weight)
    bias_both = jnp.concatenate([enc_bias, other_core(enc_bias)])

    first = 2 * half * zh + half * co
    q = lax.dynamic_slice_in_dim(query, first, half, 0)
    q = q.reshape(half, kv_local, group, head_dim).transpose(1, 2, 0, 3)
    q = q.reshape(kv_local, group * half, head_dim)
    lens = lax.dynamic_index_in_dim(lengths, zh, 0, keepdims=False)
    ids = jnp.arange(lens.shape[0], dtype=jnp.int32)
    offsets = jnp.sum(jnp.where(ids[None, :] < ids[:, None], lens[None, :], 0), axis=1)
    slot_ids = jnp.arange(slots, dtype=jnp.int32)
    shard = ((zl * 2 + jnp.stack([co, 1 - co])[:, None]) * 4 + turn[None, :]) * 4 + y
    pick = shard[..., None] == ids
    own_offset = jnp.sum(jnp.where(pick, offsets, 0), axis=-1)[..., None]
    own_len = jnp.sum(jnp.where(pick, lens, 0), axis=-1)[..., None]
    key_pos = jnp.where(slot_ids < own_len, own_offset + slot_ids, 1 << 30)
    row_pos = lax.dynamic_slice_in_dim(query_pos, first, half, 0)
    row_pos = jnp.broadcast_to(row_pos[None, :], (group, half)).reshape(-1, 1)

    message = pl.pallas_call(
        attend, out_shape=jax.ShapeDtypeStruct((8, 2 * half, 2 * HD), BF16), name="attend"
    )(q, kv, kv_other, key_pos.reshape(1, -1), row_pos)
    message = exchanged(message, (ZL, Y))
    attention = pl.pallas_call(
        combine, out_shape=jax.ShapeDtypeStruct((half, 2 * HD), BF16), name="combine"
    )(message)
    ring = [attention] + [shifted(attention, ZH, k) for k in (1, 2, 3)]
    part = pl.pallas_call(
        project,
        out_shape=jax.ShapeDtypeStruct((8, 4, half // 2, 4 * cols), BF16),
        in_specs=[pl.BlockSpec(memory_space=pltpu.SMEM)]
        + [pl.BlockSpec(memory_space=pltpu.VMEM)] * 8,
        name="project",
    )(jnp.stack([zh, co]), *ring, proj_mine, proj_other, res_mine, res_other)
    part = exchanged(part.reshape(32, half // 2, 4 * cols), (ZL, Y, X))
    piece = jnp.sum(part.astype(F32), axis=0).astype(BF16)

    my_rows = seqs * half
    wide = feats // 2
    few = my_rows // 16
    block = gathered(piece, (ZH, ZL, Y)).reshape(4, my_rows, 4 * cols)

    def encoded(weight):
        return jnp.einsum(
            "zrf,zfc->rc", block, weight.reshape(4, feats // 4, lat), preferred_element_type=F32
        )

    part = jnp.concatenate([encoded(enc_weight), encoded(enc_other)], axis=1)
    low = part.astype(BF16)
    preact = part + sum(shifted(low, X, k).astype(F32) for k in (1, 2, 3)) + bias_both
    latents = (jax.nn.softplus(4.0 * preact) * 0.25).astype(BF16)

    block_other = other_core(block)
    latents_other = other_core(latents[:, lat:])
    halves = [lax.dynamic_index_in_dim(b, zh, 0, keepdims=False) for b in (block, block_other)]
    spot = (half * (2 * zl + co), cols * y)
    halves = [lax.dynamic_slice(b, spot, (half, cols)) for b in halves]
    halves = [jnp.where(co == 0, halves[0], halves[1]), jnp.where(co == 0, halves[1], halves[0])]
    layer_out = lax.ppermute(
        jnp.concatenate(halves, axis=0),
        (ZL, CO, X),
        [(b * 4 + a, a * 4 + b) for a in range(4) for b in range(4)],
    )

    def decoded(k):
        piece = slice(k * wide, (k + 1) * wide)
        return dot(latents[:, :lat], dec_weight[:, piece], ((1,), (0,))) + dot(
            latents[:, lat:], dec_other[:, piece], ((1,), (0,))
        )

    recon = jnp.stack([decoded(0), decoded(1)]).astype(BF16).reshape(32, few, wide)
    recon = jnp.sum(exchanged(recon, (ZL, ZH, Y)).astype(F32), axis=0)
    at = (zl * 4 + zh) * 4 + y
    natural = block.transpose(1, 0, 2).reshape(my_rows, feats)
    target = lax.dynamic_slice(natural, (few * (at % 16), wide * (at // 16)), (few, wide))
    target_bias = lax.dynamic_slice_in_dim(dec_bias, wide * (at // 16), wide, 0)
    error = ((recon + target_bias - target.astype(F32)) * rows ** (-0.5)).astype(BF16)
    error = gathered(error, (ZL, ZH, Y)).reshape(2, my_rows, wide)
    error_other = other_core(error)

    def pulled(weight):
        return sum(
            dot(error[k], weight[:, k * wide : (k + 1) * wide], ((1,), (1,))) for k in (0, 1)
        )

    part = jnp.concatenate([pulled(dec_weight), pulled(dec_other)], axis=1)
    low = part.astype(BF16)
    latent_grad = part + sum(shifted(low, X, k).astype(F32) for k in (1, 2, 3))
    preact_grad = (latent_grad * jax.nn.sigmoid(4.0 * preact)).astype(BF16)
    preact_grad_other = other_core(preact_grad[:, lat:])
    preact_grad = preact_grad[:, :lat]

    all_latents = jnp.concatenate([latents[:, :lat], latents_other], axis=0)
    all_error = jnp.concatenate([error, error_other], axis=1)
    all_error = all_error.transpose(1, 0, 2).reshape(rows, feats)
    dec_grad = dot(all_latents, all_error, ((0,), (0,))).astype(BF16)
    dec_bias_grad = jnp.sum(all_error, axis=0, dtype=F32)
    all_grad = jnp.concatenate([preact_grad, preact_grad_other], axis=0)
    all_block = jnp.concatenate([block, block_other], axis=1)
    enc_grad = jnp.einsum("zrf,rc->zfc", all_block, all_grad, preferred_element_type=F32)
    enc_grad = enc_grad.astype(BF16).reshape(feats, lat)
    enc_bias_grad = jnp.sum(all_grad, axis=0, dtype=F32)
    return (layer_out, enc_grad, enc_bias_grad, dec_grad, dec_bias_grad)


def solution(mesh):
    torus = Mesh(mesh.devices.reshape(2, 2, 4, 4, mesh.shape["wid"]), (ZL, CO, ZH, Y, X))
    in_specs = (
        P(None, X, None),
        P(None, SHARD, X, None),
        P(None, SHARD, X, None),
        P(),
        P(),
        P(X, SHARD),
        P(X, SHARD),
        P(X, SHARD),
        P(SHARD),
        P(SHARD, X),
        P(X),
    )
    out_specs = (P(X, SHARD), P(X, SHARD), P(SHARD), P(SHARD, X), P(X))
    return jax.shard_map(body, mesh=torus, in_specs=in_specs, out_specs=out_specs, check_vma=False)
```

```python
import jax
import jax.numpy as jnp
from jax import lax
from jax.experimental import pallas as pl
from jax.experimental.pallas import tpu as pltpu
from jax.sharding import Mesh
from jax.sharding import PartitionSpec as P

HD = 128
ZL, CO, ZH, Y, X = ("zl", "co", "zh", "y", "x")
SHARD = (ZL, CO, ZH, Y)
F32, BF16 = (jnp.float32, jnp.bfloat16)


def other_core(a):
    return lax.ppermute(a, CO, [(0, 1), (1, 0)])


def shifted(a, axis, k):
    n = lax.axis_size(axis)
    return lax.ppermute(a, axis, [(i, (i + k) % n) for i in range(n)])


def exchanged(a, axes):
    return lax.all_to_all(a, axes, 0, 0, tiled=True)


def gathered(a, axes):
    return exchanged(jnp.broadcast_to(a, (lax.axis_size(axes), *a.shape)), axes)


def dot(a, b, contract):
    return lax.dot_general(a, b, (contract, ((), ())), preferred_element_type=F32)


def attend(q_ref, kv_ref, other_ref, key_ref, row_ref, proj_ref, out_ref):
    rest = proj_ref.shape[1]
    few = out_ref.shape[1] - rest
    out_ref[:, few:] = proj_ref[...]
    slots = kv_ref.shape[1] // 2
    visible = key_ref[...] <= row_ref[...]
    lane = lax.broadcasted_iota(jnp.int32, (q_ref.shape[1], HD), 1)
    for k in range(q_ref.shape[0]):
        across = slice(k * HD, (k + 1) * HD)
        keys, values = (
            jnp.concatenate([ref[j, lo : lo + slots, across] for ref in (kv_ref, other_ref) for j in range(4)])
            for lo in (0, slots)
        )
        scores = dot(q_ref[k], keys, ((1,), (1,))) * HD ** (-0.5)
        peak = jnp.max(jnp.where(visible, scores, -1e30), axis=1, keepdims=True)
        weights = jnp.where(visible, jnp.exp(scores - peak), 0.0)
        weight_sum = jnp.sum(weights, axis=1, keepdims=True)
        weighted = dot(weights.astype(BF16), values, ((1,), (0,)))
        some = weight_sum > 0.0
        safe = jnp.where(some, weight_sum, 1.0)
        level = jnp.where(some, peak + jnp.log(safe), -1e30)
        high = level.astype(BF16).astype(F32)
        mid = (level - high).astype(BF16).astype(F32)
        low = level - high - mid
        extra = jnp.where(lane == 0, high, jnp.where(lane == 1, mid, jnp.where(lane == 2, low, 0.0)))
        parts = out_ref.shape[0] // q_ref.shape[0]
        where = slice(k * parts, (k + 1) * parts)
        out_ref[where, :few, :HD] = (weighted / safe).astype(BF16).reshape(parts, -1, HD)
        out_ref[where, :few, HD:] = extra.astype(BF16).reshape(parts, -1, HD)


def combine(message_ref, out_ref):
    half = out_ref.shape[0]
    message = message_ref[:, : 2 * half].astype(F32)
    level = jnp.sum(message[:, :, HD:], axis=2, keepdims=True)
    share = jnp.exp(level - jnp.max(level, axis=0, keepdims=True))
    attention = jnp.sum(message[:, :, :HD] * share, axis=0) / jnp.sum(share, axis=0)
    out_ref[:, :HD] = attention[:half].astype(BF16)
    out_ref[:, HD:] = attention[half:].astype(BF16)


def project(at_ref, a_ref, b_ref, c_ref, d_ref, mine_ref, other_ref, res_mine_ref, res_other_ref, out_ref):
    attention = jnp.concatenate([ref[...] for ref in (a_ref, b_ref, c_ref, d_ref)])
    few, cols = (out_ref.shape[2], out_ref.shape[3] // 4)
    turn, core = (at_ref[0], at_ref[1])
    for high in range(2):
        for ref, res, low in ((mine_ref, res_mine_ref, core), (other_ref, res_other_ref, 1 - core)):
            top = ref.shape[1] - other_ref.shape[1]
            weight = jnp.concatenate([ref[4 * high + j, top : top + cols] for j in range(4)])
            out = dot(attention, weight, ((1,), (1,))) + res[high].astype(F32)
            out = out.astype(BF16)
            for k in range(4):
                seq = lax.rem(turn - k + 4, 4)
                for r in range(2):
                    start = few * (2 * k + r)
                    out_ref[2 * seq + r, 2 * high + low] = out[start : start + few]


def body(
    query,
    keys,
    values,
    lengths,
    query_pos,
    resid,
    out_weight,
    enc_weight,
    enc_bias,
    dec_weight,
    dec_bias,
):
    zl, co, zh, y, x = (lax.axis_index(name) for name in (ZL, CO, ZH, Y, X))
    seqs, slots, kv_local, head_dim = keys.shape
    rows = query.shape[0]
    heads = query.shape[1]
    group = heads // kv_local
    half = rows // seqs // 2
    width = kv_local * head_dim
    cols = out_weight.shape[1]
    lat = enc_weight.shape[1]
    feats = enc_weight.shape[0]

    kv = jnp.concatenate(
        [keys.reshape(seqs, slots, width), values.reshape(seqs, slots, width)], axis=1
    )
    ring = [lax.dynamic_index_in_dim(kv, zh, 0, keepdims=False)] + [
        shifted(lax.dynamic_index_in_dim(kv, (zh + k) % 4, 0, keepdims=False), ZH, k)
        for k in (1, 2, 3)
    ]

    proj = out_weight.reshape(8, 2 * HD, cols).transpose(0, 2, 1)
    res = jnp.pad(resid.reshape(8, 8, cols), ((0, 0), (0, 8), (0, 2 * HD - cols)))
    proj = jnp.concatenate([proj, res], axis=1)
    kv = jnp.stack(ring)
    kv_other = other_core(kv)
    turn = (zh - jnp.arange(4)) % 4

    first = 2 * half * zh + half * co
    q = lax.dynamic_slice_in_dim(query, first, half, 0)
    q = q.reshape(half, kv_local, group, head_dim).transpose(1, 2, 0, 3)
    q = q.reshape(kv_local, group * half, head_dim)
    lens = lax.dynamic_index_in_dim(lengths, zh, 0, keepdims=False)
    ids = jnp.arange(lens.shape[0], dtype=jnp.int32)
    offsets = jnp.sum(jnp.where(ids[None, :] < ids[:, None], lens[None, :], 0), axis=1)
    slot_ids = jnp.arange(slots, dtype=jnp.int32)
    shard = ((zl * 2 + jnp.stack([co, 1 - co])[:, None]) * 4 + turn[None, :]) * 4 + y
    pick = shard[..., None] == ids
    own_offset = jnp.sum(jnp.where(pick, offsets, 0), axis=-1)[..., None]
    own_len = jnp.sum(jnp.where(pick, lens, 0), axis=-1)[..., None]
    key_pos = jnp.where(slot_ids < own_len, own_offset + slot_ids, 1 << 30)
    row_pos = lax.dynamic_slice_in_dim(query_pos, first, half, 0)
    row_pos = jnp.broadcast_to(row_pos[None, :], (group, half)).reshape(-1, 1)

    message = pl.pallas_call(
        attend,
        out_shape=jax.ShapeDtypeStruct((8, 2 * half + proj.shape[1], 2 * HD), BF16),
        name="attend",
    )(q, kv, kv_other, key_pos.reshape(1, -1), row_pos, proj)
    message = exchanged(message, (ZL, Y))
    proj_mine = message[:, 2 * half :]
    proj_other = other_core(proj_mine)
    at = zl * 4 + y

    def residual(proj):
        res = proj[:, cols : cols + 8, :cols].reshape(2, 4, 8, cols)
        res = res.transpose(0, 2, 1, 3).reshape(2, 1, 1, 8, 4 * cols)
        here = (jnp.arange(4) == at % 4) & (turn == x)[:, None] & (co == at // 4)
        return jnp.where(here[None, :, :, None, None], res, 0).reshape(2, seqs * half, 4 * cols)

    res_mine, res_other = (residual(proj_mine), residual(proj_other))
    attention = pl.pallas_call(
        combine, out_shape=jax.ShapeDtypeStruct((half, 2 * HD), BF16), name="combine"
    )(message)
    ring = [attention] + [shifted(attention, ZH, k) for k in (1, 2, 3)]
    part = pl.pallas_call(
        project,
        out_shape=jax.ShapeDtypeStruct((8, 4, half // 2, 4 * cols), BF16),
        in_specs=[pl.BlockSpec(memory_space=pltpu.SMEM)]
        + [pl.BlockSpec(memory_space=pltpu.VMEM)] * 8,
        name="project",
    )(jnp.stack([zh, co]), *ring, message, proj_other, res_mine, res_other)
    part, enc_ready, dec_ready, bias_ready = lax.optimization_barrier(
        (part, enc_weight, dec_weight, enc_bias)
    )
    enc_other = other_core(enc_ready)
    dec_other = other_core(dec_ready)
    bias_other = other_core(bias_ready)
    part = exchanged(part.reshape(32, half // 2, 4 * cols), (ZL, Y, X))
    piece = jnp.sum(part.astype(F32), axis=0).astype(BF16)

    my_rows = seqs * half
    wide = feats // 2
    few = my_rows // 16
    block = gathered(piece, (ZH, ZL, Y)).reshape(4, my_rows, 4 * cols)
    block, enc_other, bias_other = lax.optimization_barrier((block, enc_other, bias_other))
    bias_both = jnp.concatenate([enc_bias, bias_other])

    def encoded(weight):
        return jnp.einsum(
            "zrf,zfc->rc", block, weight.reshape(4, feats // 4, lat), preferred_element_type=F32
        )

    part = jnp.concatenate([encoded(enc_weight), encoded(enc_other)], axis=1)
    low = part.astype(BF16)
    preact = part + sum(shifted(low, X, k).astype(F32) for k in (1, 2, 3)) + bias_both
    latents = (jax.nn.softplus(4.0 * preact) * 0.25).astype(BF16)

    natural = block.transpose(1, 0, 2).reshape(my_rows, feats)
    natural_other = other_core(natural)
    latents_other = other_core(latents[:, lat:])
    spot = (half * (2 * zl + co), 4 * cols * zh + cols * y)
    halves = [lax.dynamic_slice(b, spot, (half, cols)) for b in (natural, natural_other)]
    halves = [jnp.where(co == 0, halves[0], halves[1]), jnp.where(co == 0, halves[1], halves[0])]
    layer_out = lax.ppermute(
        jnp.concatenate(halves, axis=0),
        (ZL, CO, X),
        [(b * 4 + a, a * 4 + b) for a in range(4) for b in range(4)],
    )

    def decoded(k):
        piece = slice(k * wide, (k + 1) * wide)
        return dot(latents[:, :lat], dec_weight[:, piece], ((1,), (0,))) + dot(
            latents[:, lat:], dec_other[:, piece], ((1,), (0,))
        )

    recon = jnp.stack([decoded(0), decoded(1)]).astype(BF16).reshape(32, few, wide)
    recon = jnp.sum(exchanged(recon, (ZL, ZH, Y)).astype(F32), axis=0)
    at = (zl * 4 + zh) * 4 + y
    target = lax.dynamic_slice(natural, (few * (at % 16), wide * (at // 16)), (few, wide))
    target_bias = lax.dynamic_slice_in_dim(dec_bias, wide * (at // 16), wide, 0)
    error = ((recon + target_bias - target.astype(F32)) * rows ** (-0.5)).astype(BF16)
    error, natural_other, latents_other = lax.optimization_barrier(
        (error, natural_other, latents_other)
    )
    error = gathered(error, (ZL, ZH, Y)).reshape(2, my_rows, wide)
    all_natural = jnp.concatenate([natural, natural_other], axis=0).T
    all_latents = jnp.concatenate([latents[:, :lat], latents_other], axis=0).T
    error, layer_out, all_natural, all_latents = lax.optimization_barrier(
        (error, layer_out, all_natural, all_latents)
    )
    error_other = other_core(error)

    def pulled(weight):
        return sum(
            dot(error[k], weight[:, k * wide : (k + 1) * wide], ((1,), (1,))) for k in (0, 1)
        )

    part = jnp.concatenate([pulled(dec_weight), pulled(dec_other)], axis=1)
    low = part.astype(BF16)
    latent_grad = part + sum(shifted(low, X, k).astype(F32) for k in (1, 2, 3))
    preact_grad = (latent_grad * jax.nn.sigmoid(4.0 * preact)).astype(BF16)
    preact_grad_other = other_core(preact_grad[:, lat:])
    preact_grad = preact_grad[:, :lat]

    all_error = jnp.concatenate([error, error_other], axis=1)
    all_error = all_error.transpose(1, 0, 2).reshape(rows, feats)
    dec_grad = dot(all_latents, all_error, ((1,), (0,))).astype(BF16)
    dec_bias_grad = jnp.sum(all_error, axis=0, dtype=F32)
    all_grad = jnp.concatenate([preact_grad, preact_grad_other], axis=0)
    enc_grad = dot(all_natural, all_grad, ((1,), (0,))).astype(BF16)
    enc_bias_grad = jnp.sum(all_grad, axis=0, dtype=F32)
    return (layer_out, enc_grad, enc_bias_grad, dec_grad, dec_bias_grad)


def solution(mesh):
    torus = Mesh(mesh.devices.reshape(2, 2, 4, 4, mesh.shape["wid"]), (ZL, CO, ZH, Y, X))
    in_specs = (
        P(None, X, None),
        P(None, SHARD, X, None),
        P(None, SHARD, X, None),
        P(),
        P(),
        P(X, SHARD),
        P(X, SHARD),
        P(X, SHARD),
        P(SHARD),
        P(SHARD, X),
        P(X),
    )
    out_specs = (P(X, SHARD), P(X, SHARD), P(SHARD), P(SHARD, X), P(X))
    return jax.shard_map(body, mesh=torus, in_specs=in_specs, out_specs=out_specs, check_vma=False)
```

```python
import jax
import jax.numpy as jnp
from jax import lax
from jax.experimental import pallas as pl
from jax.experimental.pallas import tpu as pltpu
from jax.sharding import Mesh
from jax.sharding import PartitionSpec as P

HD = 128
ZL, CO, ZH, Y, X = ("zl", "co", "zh", "y", "x")
SHARD = (ZL, CO, ZH, Y)
F32, BF16 = (jnp.float32, jnp.bfloat16)


def other_core(a):
    return lax.ppermute(a, CO, [(0, 1), (1, 0)])


def shifted(a, axis, k):
    n = lax.axis_size(axis)
    return lax.ppermute(a, axis, [(i, (i + k) % n) for i in range(n)])


def exchanged(a, axes):
    return lax.all_to_all(a, axes, 0, 0, tiled=True)


def gathered(a, axes):
    return exchanged(jnp.broadcast_to(a, (lax.axis_size(axes), *a.shape)), axes)


def dot(a, b, contract):
    return lax.dot_general(a, b, (contract, ((), ())), preferred_element_type=F32)


def attend(q_ref, kv_ref, other_ref, key_ref, row_ref, proj_ref, out_ref):
    rest = proj_ref.shape[1]
    few = out_ref.shape[1] - rest
    out_ref[:, few:] = proj_ref[...]
    slots = kv_ref.shape[1] // 2
    visible = key_ref[...] <= row_ref[...]
    lane = lax.broadcasted_iota(jnp.int32, (q_ref.shape[1], HD), 1)
    for k in range(q_ref.shape[0]):
        across = slice(k * HD, (k + 1) * HD)
        keys, values = (
            jnp.concatenate([ref[j, lo : lo + slots, across] for ref in (kv_ref, other_ref) for j in range(4)])
            for lo in (0, slots)
        )
        scores = dot(q_ref[k], keys, ((1,), (1,))) * HD ** (-0.5)
        peak = jnp.max(jnp.where(visible, scores, -1e30), axis=1, keepdims=True)
        weights = jnp.where(visible, jnp.exp(scores - peak), 0.0)
        weight_sum = jnp.sum(weights, axis=1, keepdims=True)
        weighted = dot(weights.astype(BF16), values, ((1,), (0,)))
        some = weight_sum > 0.0
        safe = jnp.where(some, weight_sum, 1.0)
        level = jnp.where(some, peak + jnp.log(safe), -1e30)
        high = level.astype(BF16).astype(F32)
        mid = (level - high).astype(BF16).astype(F32)
        low = level - high - mid
        extra = jnp.where(lane == 0, high, jnp.where(lane == 1, mid, jnp.where(lane == 2, low, 0.0)))
        parts = out_ref.shape[0] // q_ref.shape[0]
        where = slice(k * parts, (k + 1) * parts)
        out_ref[where, :few, :HD] = (weighted / safe).astype(BF16).reshape(parts, -1, HD)
        out_ref[where, :few, HD:] = extra.astype(BF16).reshape(parts, -1, HD)


def combine(message_ref, out_ref):
    half = out_ref.shape[0]
    message = message_ref[:, : 2 * half].astype(F32)
    level = jnp.sum(message[:, :, HD:], axis=2, keepdims=True)
    share = jnp.exp(level - jnp.max(level, axis=0, keepdims=True))
    attention = jnp.sum(message[:, :, :HD] * share, axis=0) / jnp.sum(share, axis=0)
    out_ref[:, :HD] = attention[:half].astype(BF16)
    out_ref[:, HD:] = attention[half:].astype(BF16)


def project(at_ref, a_ref, b_ref, c_ref, d_ref, mine_ref, other_ref, res_mine_ref, res_other_ref, out_ref):
    attention = jnp.concatenate([ref[...] for ref in (a_ref, b_ref, c_ref, d_ref)])
    few, cols = (out_ref.shape[2], out_ref.shape[3] // 4)
    turn, core = (at_ref[0], at_ref[1])
    for high in range(2):
        for ref, res, low in ((mine_ref, res_mine_ref, core), (other_ref, res_other_ref, 1 - core)):
            top = ref.shape[1] - other_ref.shape[1]
            weight = jnp.concatenate([ref[4 * high + j, top : top + cols] for j in range(4)])
            out = dot(attention, weight, ((1,), (1,))) + res[high].astype(F32)
            out = out.astype(BF16)
            for k in range(4):
                seq = lax.rem(turn - k + 4, 4)
                for r in range(2):
                    start = few * (2 * k + r)
                    out_ref[2 * seq + r, 2 * high + low] = out[start : start + few]


def body(
    query,
    keys,
    values,
    lengths,
    query_pos,
    resid,
    out_weight,
    enc_weight,
    enc_bias,
    dec_weight,
    dec_bias,
):
    zl, co, zh, y, x = (lax.axis_index(name) for name in (ZL, CO, ZH, Y, X))
    seqs, slots, kv_local, head_dim = keys.shape
    rows = query.shape[0]
    heads = query.shape[1]
    group = heads // kv_local
    half = rows // seqs // 2
    width = kv_local * head_dim
    cols = out_weight.shape[1]
    lat = enc_weight.shape[1]
    feats = enc_weight.shape[0]

    kv = jnp.concatenate(
        [keys.reshape(seqs, slots, width), values.reshape(seqs, slots, width)], axis=1
    )
    ring = [lax.dynamic_index_in_dim(kv, zh, 0, keepdims=False)] + [
        shifted(lax.dynamic_index_in_dim(kv, (zh + k) % 4, 0, keepdims=False), ZH, k)
        for k in (1, 2, 3)
    ]

    proj = out_weight.reshape(8, 2 * HD, cols).transpose(0, 2, 1)
    res = jnp.pad(resid.reshape(8, 8, cols), ((0, 0), (0, 8), (0, 2 * HD - cols)))
    proj = jnp.concatenate([proj, res], axis=1)
    kv = jnp.stack(ring)
    kv_other = other_core(kv)
    turn = (zh - jnp.arange(4)) % 4

    first = 2 * half * zh + half * co
    q = lax.dynamic_slice_in_dim(query, first, half, 0)
    q = q.reshape(half, kv_local, group, head_dim).transpose(1, 2, 0, 3)
    q = q.reshape(kv_local, group * half, head_dim)
    lens = lax.dynamic_index_in_dim(lengths, zh, 0, keepdims=False)
    ids = jnp.arange(lens.shape[0], dtype=jnp.int32)
    offsets = jnp.sum(jnp.where(ids[None, :] < ids[:, None], lens[None, :], 0), axis=1)
    slot_ids = jnp.arange(slots, dtype=jnp.int32)
    shard = ((zl * 2 + jnp.stack([co, 1 - co])[:, None]) * 4 + turn[None, :]) * 4 + y
    pick = shard[..., None] == ids
    own_offset = jnp.sum(jnp.where(pick, offsets, 0), axis=-1)[..., None]
    own_len = jnp.sum(jnp.where(pick, lens, 0), axis=-1)[..., None]
    key_pos = jnp.where(slot_ids < own_len, own_offset + slot_ids, 1 << 30)
    row_pos = lax.dynamic_slice_in_dim(query_pos, first, half, 0)
    row_pos = jnp.broadcast_to(row_pos[None, :], (group, half)).reshape(-1, 1)

    message = pl.pallas_call(
        attend,
        out_shape=jax.ShapeDtypeStruct((8, 2 * half + proj.shape[1], 2 * HD), BF16),
        name="attend",
    )(q, kv, kv_other, key_pos.reshape(1, -1), row_pos, proj)
    message, enc_ready, bias_ready = lax.optimization_barrier(
        (message, enc_weight, enc_bias)
    )
    enc_other = other_core(enc_ready)
    bias_other = other_core(bias_ready)
    message = exchanged(message, (ZL, Y))
    message, enc_other, bias_other = lax.optimization_barrier((message, enc_other, bias_other))
    proj_mine = message[:, 2 * half :]
    proj_other = other_core(proj_mine)
    at = zl * 4 + y

    def residual(proj):
        res = proj[:, cols : cols + 8, :cols].reshape(2, 4, 8, cols)
        res = res.transpose(0, 2, 1, 3).reshape(2, 1, 1, 8, 4 * cols)
        here = (jnp.arange(4) == at % 4) & (turn == x)[:, None] & (co == at // 4)
        return jnp.where(here[None, :, :, None, None], res, 0).reshape(2, seqs * half, 4 * cols)

    res_mine, res_other = (residual(proj_mine), residual(proj_other))
    attention = pl.pallas_call(
        combine, out_shape=jax.ShapeDtypeStruct((half, 2 * HD), BF16), name="combine"
    )(message)
    ring = [attention] + [shifted(attention, ZH, k) for k in (1, 2, 3)]
    part = pl.pallas_call(
        project,
        out_shape=jax.ShapeDtypeStruct((8, 4, half // 2, 4 * cols), BF16),
        in_specs=[pl.BlockSpec(memory_space=pltpu.SMEM)]
        + [pl.BlockSpec(memory_space=pltpu.VMEM)] * 8,
        name="project",
    )(jnp.stack([zh, co]), *ring, message, proj_other, res_mine, res_other)
    part, dec_ready = lax.optimization_barrier((part, dec_weight))
    dec_other = other_core(dec_ready)
    part = exchanged(part.reshape(32, half // 2, 4 * cols), (ZL, Y, X))
    piece = jnp.sum(part.astype(F32), axis=0).astype(BF16)

    my_rows = seqs * half
    wide = feats // 2
    few = my_rows // 16
    block = gathered(piece, (ZH, ZL, Y)).reshape(4, my_rows, 4 * cols)
    block, enc_other, bias_other = lax.optimization_barrier((block, enc_other, bias_other))
    bias_both = jnp.concatenate([enc_bias, bias_other])

    def encoded(weight):
        return jnp.einsum(
            "zrf,zfc->rc", block, weight.reshape(4, feats // 4, lat), preferred_element_type=F32
        )

    part = jnp.concatenate([encoded(enc_weight), encoded(enc_other)], axis=1)
    low = part.astype(BF16)
    preact = part + sum(shifted(low, X, k).astype(F32) for k in (1, 2, 3)) + bias_both
    latents = (jax.nn.softplus(4.0 * preact) * 0.25).astype(BF16)

    natural = block.transpose(1, 0, 2).reshape(my_rows, feats)
    natural_other = other_core(natural)
    latents_other = other_core(latents[:, lat:])
    spot = (half * (2 * zl + co), 4 * cols * zh + cols * y)
    halves = [lax.dynamic_slice(b, spot, (half, cols)) for b in (natural, natural_other)]
    halves = [jnp.where(co == 0, halves[0], halves[1]), jnp.where(co == 0, halves[1], halves[0])]
    layer_out = lax.ppermute(
        jnp.concatenate(halves, axis=0),
        (ZL, CO, X),
        [(b * 4 + a, a * 4 + b) for a in range(4) for b in range(4)],
    )

    def decoded(k):
        piece = slice(k * wide, (k + 1) * wide)
        return dot(latents[:, :lat], dec_weight[:, piece], ((1,), (0,))) + dot(
            latents[:, lat:], dec_other[:, piece], ((1,), (0,))
        )

    recon = jnp.stack([decoded(0), decoded(1)]).astype(BF16).reshape(32, few, wide)
    recon = jnp.sum(exchanged(recon, (ZL, ZH, Y)).astype(F32), axis=0)
    at = (zl * 4 + zh) * 4 + y
    target = lax.dynamic_slice(natural, (few * (at % 16), wide * (at // 16)), (few, wide))
    target_bias = lax.dynamic_slice_in_dim(dec_bias, wide * (at // 16), wide, 0)
    error = ((recon + target_bias - target.astype(F32)) * rows ** (-0.5)).astype(BF16)
    error, natural_other, latents_other = lax.optimization_barrier(
        (error, natural_other, latents_other)
    )
    error = gathered(error, (ZL, ZH, Y)).reshape(2, my_rows, wide)
    all_natural = jnp.concatenate([natural, natural_other], axis=0).T
    all_latents = jnp.concatenate([latents[:, :lat], latents_other], axis=0).T
    error, layer_out, all_natural, all_latents = lax.optimization_barrier(
        (error, layer_out, all_natural, all_latents)
    )
    error_other = other_core(error)

    def pulled(weight):
        return sum(
            dot(error[k], weight[:, k * wide : (k + 1) * wide], ((1,), (1,))) for k in (0, 1)
        )

    part = jnp.concatenate([pulled(dec_weight), pulled(dec_other)], axis=1)
    low = part.astype(BF16)
    latent_grad = part + sum(shifted(low, X, k).astype(F32) for k in (1, 2, 3))
    preact_grad = (latent_grad * jax.nn.sigmoid(4.0 * preact)).astype(BF16)
    preact_grad_other = other_core(preact_grad[:, lat:])
    preact_grad = preact_grad[:, :lat]

    all_error = jnp.concatenate([error, error_other], axis=1)
    all_error = all_error.transpose(1, 0, 2).reshape(rows, feats)
    dec_grad = dot(all_latents, all_error, ((1,), (0,))).astype(BF16)
    dec_bias_grad = jnp.sum(all_error, axis=0, dtype=F32)
    all_grad = jnp.concatenate([preact_grad, preact_grad_other], axis=0)
    enc_grad = dot(all_natural, all_grad, ((1,), (0,))).astype(BF16)
    enc_bias_grad = jnp.sum(all_grad, axis=0, dtype=F32)
    return (layer_out, enc_grad, enc_bias_grad, dec_grad, dec_bias_grad)


def solution(mesh):
    torus = Mesh(mesh.devices.reshape(2, 2, 4, 4, mesh.shape["wid"]), (ZL, CO, ZH, Y, X))
    in_specs = (
        P(None, X, None),
        P(None, SHARD, X, None),
        P(None, SHARD, X, None),
        P(),
        P(),
        P(X, SHARD),
        P(X, SHARD),
        P(X, SHARD),
        P(SHARD),
        P(SHARD, X),
        P(X),
    )
    out_specs = (P(X, SHARD), P(X, SHARD), P(SHARD), P(SHARD, X), P(X))
    return jax.shard_map(body, mesh=torus, in_specs=in_specs, out_specs=out_specs, check_vma=False)
```

```python
import jax
import jax.numpy as jnp
from jax import lax
from jax.experimental import pallas as pl
from jax.experimental.pallas import tpu as pltpu
from jax.sharding import Mesh
from jax.sharding import PartitionSpec as P

HD = 128
ZL, CO, ZH, Y, X = ("zl", "co", "zh", "y", "x")
SHARD = (ZL, CO, ZH, Y)
F32, BF16 = (jnp.float32, jnp.bfloat16)


def other_core(a):
    return lax.ppermute(a, CO, [(0, 1), (1, 0)])


def shifted(a, axis, k):
    n = lax.axis_size(axis)
    return lax.ppermute(a, axis, [(i, (i + k) % n) for i in range(n)])


def exchanged(a, axes):
    return lax.all_to_all(a, axes, 0, 0, tiled=True)


def gathered(a, axes):
    return exchanged(jnp.broadcast_to(a, (lax.axis_size(axes), *a.shape)), axes)


def dot(a, b, contract):
    return lax.dot_general(a, b, (contract, ((), ())), preferred_element_type=F32)


def attend(q_ref, kv_ref, other_ref, key_ref, row_ref, proj_ref, out_ref):
    rest = proj_ref.shape[1]
    few = out_ref.shape[1] - rest
    out_ref[:, few:] = proj_ref[...]
    slots = kv_ref.shape[1] // 2
    visible = key_ref[...] <= row_ref[...]
    lane = lax.broadcasted_iota(jnp.int32, (q_ref.shape[1], HD), 1)
    for k in range(q_ref.shape[0]):
        across = slice(k * HD, (k + 1) * HD)
        keys, values = (
            jnp.concatenate([ref[j, lo : lo + slots, across] for ref in (kv_ref, other_ref) for j in range(4)])
            for lo in (0, slots)
        )
        scores = dot(q_ref[k], keys, ((1,), (1,))) * HD ** (-0.5)
        peak = jnp.max(jnp.where(visible, scores, -1e30), axis=1, keepdims=True)
        weights = jnp.where(visible, jnp.exp(scores - peak), 0.0)
        weight_sum = jnp.sum(weights, axis=1, keepdims=True)
        weighted = dot(weights.astype(BF16), values, ((1,), (0,)))
        some = weight_sum > 0.0
        safe = jnp.where(some, weight_sum, 1.0)
        level = jnp.where(some, peak + jnp.log(safe), -1e30)
        high = level.astype(BF16).astype(F32)
        mid = (level - high).astype(BF16).astype(F32)
        low = level - high - mid
        extra = jnp.where(lane == 0, high, jnp.where(lane == 1, mid, jnp.where(lane == 2, low, 0.0)))
        parts = out_ref.shape[0] // q_ref.shape[0]
        where = slice(k * parts, (k + 1) * parts)
        out_ref[where, :few, :HD] = (weighted / safe).astype(BF16).reshape(parts, -1, HD)
        out_ref[where, :few, HD:] = extra.astype(BF16).reshape(parts, -1, HD)


def combine(message_ref, out_ref):
    half = out_ref.shape[0]
    message = message_ref[:, : 2 * half].astype(F32)
    level = jnp.sum(message[:, :, HD:], axis=2, keepdims=True)
    share = jnp.exp(level - jnp.max(level, axis=0, keepdims=True))
    attention = jnp.sum(message[:, :, :HD] * share, axis=0) / jnp.sum(share, axis=0)
    out_ref[:, :HD] = attention[:half].astype(BF16)
    out_ref[:, HD:] = attention[half:].astype(BF16)


def project(a_ref, b_ref, c_ref, d_ref, mine_ref, other_ref, res_mine_ref, res_other_ref, out_ref):
    attention = jnp.concatenate([ref[...] for ref in (a_ref, b_ref, c_ref, d_ref)])
    few, cols = (out_ref.shape[2], out_ref.shape[3] // 4)
    turn, core = (lax.axis_index(ZH), lax.axis_index(CO))
    for high in range(2):
        for ref, res, low in ((mine_ref, res_mine_ref, core), (other_ref, res_other_ref, 1 - core)):
            top = ref.shape[1] - other_ref.shape[1]
            weight = jnp.concatenate([ref[4 * high + j, top : top + cols] for j in range(4)])
            out = dot(attention, weight, ((1,), (1,))) + res[high].astype(F32)
            out = out.astype(BF16)
            for k in range(4):
                seq = lax.rem(turn - k + 4, 4)
                for r in range(2):
                    start = few * (2 * k + r)
                    out_ref[2 * seq + r, 2 * high + low] = out[start : start + few]


def body(
    query,
    keys,
    values,
    lengths,
    query_pos,
    resid,
    out_weight,
    enc_weight,
    enc_bias,
    dec_weight,
    dec_bias,
):
    zl, co, zh, y, x = (lax.axis_index(name) for name in (ZL, CO, ZH, Y, X))
    seqs, slots, kv_local, head_dim = keys.shape
    rows = query.shape[0]
    heads = query.shape[1]
    group = heads // kv_local
    half = rows // seqs // 2
    width = kv_local * head_dim
    cols = out_weight.shape[1]
    lat = enc_weight.shape[1]
    feats = enc_weight.shape[0]

    kv = jnp.concatenate(
        [keys.reshape(seqs, slots, width), values.reshape(seqs, slots, width)], axis=1
    )
    ring = [lax.dynamic_index_in_dim(kv, zh, 0, keepdims=False)] + [
        shifted(lax.dynamic_index_in_dim(kv, (zh + k) % 4, 0, keepdims=False), ZH, k)
        for k in (1, 2, 3)
    ]

    proj = out_weight.reshape(8, 2 * HD, cols).transpose(0, 2, 1)
    res = jnp.pad(resid.reshape(8, 8, cols), ((0, 0), (0, 8), (0, 2 * HD - cols)))
    proj = jnp.concatenate([proj, res], axis=1)
    kv = jnp.stack(ring)
    kv_other = other_core(kv)
    turn = (zh - jnp.arange(4)) % 4

    first = 2 * half * zh + half * co
    q = lax.dynamic_slice_in_dim(query, first, half, 0)
    q = q.reshape(half, kv_local, group, head_dim).transpose(1, 2, 0, 3)
    q = q.reshape(kv_local, group * half, head_dim)
    lens = lax.dynamic_index_in_dim(lengths, zh, 0, keepdims=False)
    ids = jnp.arange(lens.shape[0], dtype=jnp.int32)
    offsets = jnp.sum(jnp.where(ids[None, :] < ids[:, None], lens[None, :], 0), axis=1)
    slot_ids = jnp.arange(slots, dtype=jnp.int32)
    shard = ((zl * 2 + jnp.stack([co, 1 - co])[:, None]) * 4 + turn[None, :]) * 4 + y
    pick = shard[..., None] == ids
    own_offset = jnp.sum(jnp.where(pick, offsets, 0), axis=-1)[..., None]
    own_len = jnp.sum(jnp.where(pick, lens, 0), axis=-1)[..., None]
    key_pos = jnp.where(slot_ids < own_len, own_offset + slot_ids, 1 << 30)
    row_pos = lax.dynamic_slice_in_dim(query_pos, first, half, 0)
    row_pos = jnp.broadcast_to(row_pos[None, :], (group, half)).reshape(-1, 1)

    message = pl.pallas_call(
        attend,
        out_shape=jax.ShapeDtypeStruct((8, 2 * half + proj.shape[1], 2 * HD), BF16),
        name="attend",
    )(q, kv, kv_other, key_pos.reshape(1, -1), row_pos, proj)
    message, enc_ready, bias_ready = lax.optimization_barrier(
        (message, enc_weight, enc_bias)
    )
    enc_other = other_core(enc_ready)
    bias_other = other_core(bias_ready)
    message = exchanged(message, (ZL, Y))
    message, enc_other, bias_other = lax.optimization_barrier((message, enc_other, bias_other))
    proj_mine = message[:, 2 * half :]
    proj_other = other_core(proj_mine)
    at = zl * 4 + y

    def residual(proj):
        res = proj[:, cols : cols + 8, :cols].reshape(2, 4, 8, cols)
        res = res.transpose(0, 2, 1, 3).reshape(2, 1, 1, 8, 4 * cols)
        here = (jnp.arange(4) == at % 4) & (turn == x)[:, None] & (co == at // 4)
        return jnp.where(here[None, :, :, None, None], res, 0).reshape(2, seqs * half, 4 * cols)

    res_mine, res_other = (residual(proj_mine), residual(proj_other))
    attention = pl.pallas_call(
        combine, out_shape=jax.ShapeDtypeStruct((half, 2 * HD), BF16), name="combine"
    )(message)
    ring = [attention] + [shifted(attention, ZH, k) for k in (1, 2, 3)]
    part = pl.pallas_call(
        project,
        out_shape=jax.ShapeDtypeStruct((8, 4, half // 2, 4 * cols), BF16),
        name="project",
    )(*ring, message, proj_other, res_mine, res_other)
    part, dec_ready = lax.optimization_barrier((part, dec_weight))
    dec_other = other_core(dec_ready)
    part = exchanged(part.reshape(32, half // 2, 4 * cols), (ZL, Y, X))
    piece = jnp.sum(part.astype(F32), axis=0).astype(BF16)

    my_rows = seqs * half
    wide = feats // 2
    few = my_rows // 16
    block = gathered(piece, (ZH, ZL, Y)).reshape(4, my_rows, 4 * cols)
    block, enc_other, bias_other = lax.optimization_barrier((block, enc_other, bias_other))
    bias_both = jnp.concatenate([enc_bias, bias_other])

    def encoded(weight):
        return jnp.einsum(
            "zrf,zfc->rc", block, weight.reshape(4, feats // 4, lat), preferred_element_type=F32
        )

    part = jnp.concatenate([encoded(enc_weight), encoded(enc_other)], axis=1)
    low = part.astype(BF16)
    preact = part + sum(shifted(low, X, k).astype(F32) for k in (1, 2, 3)) + bias_both
    latents = (jax.nn.softplus(4.0 * preact) * 0.25).astype(BF16)

    natural = block.transpose(1, 0, 2).reshape(my_rows, feats)
    natural_other = other_core(natural)
    latents_other = other_core(latents[:, lat:])
    spot = (half * (2 * zl + co), 4 * cols * zh + cols * y)
    halves = [lax.dynamic_slice(b, spot, (half, cols)) for b in (natural, natural_other)]
    halves = [jnp.where(co == 0, halves[0], halves[1]), jnp.where(co == 0, halves[1], halves[0])]
    layer_out = lax.ppermute(
        jnp.concatenate(halves, axis=0),
        (ZL, CO, X),
        [(b * 4 + a, a * 4 + b) for a in range(4) for b in range(4)],
    )

    def decoded(k):
        piece = slice(k * wide, (k + 1) * wide)
        return dot(latents[:, :lat], dec_weight[:, piece], ((1,), (0,))) + dot(
            latents[:, lat:], dec_other[:, piece], ((1,), (0,))
        )

    recon = jnp.stack([decoded(0), decoded(1)]).astype(BF16).reshape(32, few, wide)
    recon = jnp.sum(exchanged(recon, (ZL, ZH, Y)).astype(F32), axis=0)
    at = (zl * 4 + zh) * 4 + y
    target = lax.dynamic_slice(natural, (few * (at % 16), wide * (at // 16)), (few, wide))
    target_bias = lax.dynamic_slice_in_dim(dec_bias, wide * (at // 16), wide, 0)
    error = ((recon + target_bias - target.astype(F32)) * rows ** (-0.5)).astype(BF16)
    error, natural_other, latents_other = lax.optimization_barrier(
        (error, natural_other, latents_other)
    )
    error = gathered(error, (ZL, ZH, Y)).reshape(2, my_rows, wide)
    all_natural = jnp.concatenate([natural, natural_other], axis=0).T
    all_latents = jnp.concatenate([latents[:, :lat], latents_other], axis=0).T
    error, layer_out, all_natural, all_latents = lax.optimization_barrier(
        (error, layer_out, all_natural, all_latents)
    )
    error_other = other_core(error)

    def pulled(weight):
        return sum(
            dot(error[k], weight[:, k * wide : (k + 1) * wide], ((1,), (1,))) for k in (0, 1)
        )

    part = jnp.concatenate([pulled(dec_weight), pulled(dec_other)], axis=1)
    low = part.astype(BF16)
    latent_grad = part + sum(shifted(low, X, k).astype(F32) for k in (1, 2, 3))
    preact_grad = (latent_grad * jax.nn.sigmoid(4.0 * preact)).astype(BF16)
    preact_grad_other = other_core(preact_grad[:, lat:])
    preact_grad = preact_grad[:, :lat]

    all_error = jnp.concatenate([error, error_other], axis=1)
    all_error = all_error.transpose(1, 0, 2).reshape(rows, feats)
    dec_grad = dot(all_latents, all_error, ((1,), (0,))).astype(BF16)
    dec_bias_grad = jnp.sum(all_error, axis=0, dtype=F32)
    all_grad = jnp.concatenate([preact_grad, preact_grad_other], axis=0)
    enc_grad = dot(all_natural, all_grad, ((1,), (0,))).astype(BF16)
    enc_bias_grad = jnp.sum(all_grad, axis=0, dtype=F32)
    return (layer_out, enc_grad, enc_bias_grad, dec_grad, dec_bias_grad)


def solution(mesh):
    torus = Mesh(mesh.devices.reshape(2, 2, 4, 4, mesh.shape["wid"]), (ZL, CO, ZH, Y, X))
    in_specs = (
        P(None, X, None),
        P(None, SHARD, X, None),
        P(None, SHARD, X, None),
        P(),
        P(),
        P(X, SHARD),
        P(X, SHARD),
        P(X, SHARD),
        P(SHARD),
        P(SHARD, X),
        P(X),
    )
    out_specs = (P(X, SHARD), P(X, SHARD), P(SHARD), P(SHARD, X), P(X))
    return jax.shard_map(body, mesh=torus, in_specs=in_specs, out_specs=out_specs, check_vma=False)
```
